128 devices in a mesh: body: 8 (over y, core), blk: 16 (over z, x).
Axes of the slice: x: 4, y: 4, z: 4, core: 2. Of those that a mesh axis runs over, the one named last changes fastest.
Arguments:
- psi_init: float32 [65536, 320], P(('body', 'blk')), may hold values from -6 to 6
- source: float32 [65536, 320], P(('body', 'blk'))
- coupling: bfloat16 [65536, 6, 5, 320], P(('body', 'blk')), may hold values from -0.59765625 to 0.59765625
- diag_inv: bfloat16 [65536, 5, 320], P(('body', 'blk')), as said below
- neighbours: int32 [65536, 6], P(('body', 'blk')), may hold values from 0 to 527, as said below
- seam_perm: int32 [8, 8], P('body'), may hold values from 0 to 7, each once within a row
- fringe_src: int32 [128, 1024], P(('body', 'blk')), may hold values from 0 to 511
- fringe_dst: int32 [128, 1024], P(('body', 'blk')), may hold values from 0 to 511, as said below
- fringe_weight: float32 [128, 1024], P(('body', 'blk')), may hold values from 0.2 to 1
Outputs:
- adjoint: float32 [65536, 320], P(('body', 'blk'))
- residual: float32 [65536, 320], P(('body', 'blk'))
The draws below stay inside these ranges and needn't reach their ends.
Inputs may be any that keep to these rules, and one draw needn't show every extreme that they name: neighbours[i, m] - 8 - (i mod 512) lies in -8 .. 8. `fringe_dst`: every slot names a receiver block. `diag_inv`: each per-cell 5 x 5 matrix has a positive diagonal.
All inputs are finite; a program needn't handle non-finite values.
Results may differ from the reference program's by a relative error of at most 0.0003.
Values sent between devices are 32-bit elements; how exact they have to be, the bound alone decides.
A program may use at most 128 MiB of HBM per device.

```python
import math
import jax
import jax.numpy as jnp
from jax import lax

CELLS = 64
VARS = 5
BW = 320
NB = 512
K = 6
HB = 8
CAP = 8
STEPS = 2
NBT = 65536
N_BODY = 8
N_BLK = 16
DEVICES = 128


def draw_source(key, part):
    rows = jnp.arange(NBT, dtype=jnp.int32)[:, None]
    device = (rows // NB).astype(jnp.float32)
    scale = 1.5 * (1.0 + 2.0 * device / max(DEVICES - 1, 1))
    base = jnp.clip(jax.random.normal(jax.random.fold_in(key, 1), (NBT, BW), jnp.float32), -6.0, 6.0)
    return base * scale


def draw_diag_inv(key, part):
    upper = jnp.arange(VARS, dtype=jnp.int32)[None, :, None]
    lower = (jnp.arange(BW, dtype=jnp.int32) // CELLS)[None, None, :]
    diag = jnp.exp(jax.random.uniform(jax.random.fold_in(key, 1), (NBT, VARS, BW), jnp.float32, math.log(0.6), math.log(1.2)))
    off = jnp.clip(0.15 * jax.random.normal(jax.random.fold_in(key, 2), (NBT, VARS, BW), jnp.float32), -0.6, 0.6)
    return jnp.where(upper == lower, diag, off).astype(jnp.bfloat16)


def draw_neighbours(key, part):
    offset = jax.random.randint(jax.random.fold_in(key, 1), (NBT, K), -HB, HB + 1)
    local = (jnp.arange(NBT, dtype=jnp.int32) % NB)[:, None]
    slot = jnp.arange(K, dtype=jnp.int32)[None, :]
    offset = jnp.where((local == NB - 1) & (slot == 0), HB, offset)
    offset = jnp.where((local == 0) & (slot == 0), -HB, offset)
    return (local + HB + offset).astype(jnp.int32)


def draw_fringe_dst(key, part):
    cols = jnp.arange(DEVICES * CAP, dtype=jnp.int32)[None, :]
    values = jax.random.randint(jax.random.fold_in(key, 1), (DEVICES, DEVICES * CAP), 0, NB)
    values = jnp.where(cols == 0, NB - 1, values)
    return values.astype(jnp.int32)


def plant(drawn, own_key, smallest, largest):
    spot = [jax.random.randint(jax.random.fold_in(own_key, axis), (), 0, length) for axis, length in enumerate(drawn.shape)]
    main_axis = drawn.shape.index(max(drawn.shape))
    beside = spot[:main_axis] + [(spot[main_axis] + 1) % drawn.shape[main_axis]] + spot[main_axis + 1:]
    return drawn.at[tuple(spot)].set(smallest).at[tuple(beside)].set(largest)


def levels(key, extent, shards, smallest, top_value):
    def one(axis_at, parts):
        steps = jax.random.uniform(jax.random.fold_in(jax.random.fold_in(key, 6), axis_at), (parts,), jnp.float32, smallest / len(shards), top_value / len(shards))
        return jnp.repeat(jnp.exp(steps), extent[axis_at] // parts).reshape((-1,) + (1,) * (len(extent) - axis_at - 1))

    gain = one(*shards[0])
    for cut in shards[1:]:
        gain = gain * one(*cut)
    return gain


def bell_draw(key, shape, deviation, limit, shards=(), kind=jnp.bfloat16):
    factor_of = levels(key, shape, shards, -0.22, 0.18) if shards else 1.0
    array = jax.random.normal(key, shape, jnp.float32) * deviation * factor_of
    return jnp.minimum(jnp.maximum(array, -limit), limit).astype(kind)


def setup_inputs(seed: int = 0) -> dict:
    key_of = jax.random.split(jax.random.key(seed), 10)
    return {
        "psi_init": bell_draw(key_of[0], (NBT, BW), 1.0, 6.0, ((0, 128),), jnp.float32),
        "source": draw_source(jax.random.fold_in(key_of[9], 71), 0),
        "coupling": bell_draw(key_of[2], (NBT, K, VARS, BW), 0.12, 0.59765625, ((0, 128),)),
        "diag_inv": draw_diag_inv(jax.random.fold_in(key_of[9], 71), 0),
        "neighbours": draw_neighbours(jax.random.fold_in(key_of[9], 71), 0),
        "seam_perm": jax.vmap(lambda own: jax.random.permutation(own, HB))(jax.random.split(key_of[5], N_BODY)).reshape((N_BODY, HB)).astype(jnp.int32),
        "fringe_src": plant(jax.random.randint(key_of[6], (DEVICES, DEVICES * CAP), 0, NB), jax.random.fold_in(key_of[6], 1), 0, NB - 1).astype(jnp.int32),
        "fringe_dst": draw_fringe_dst(jax.random.fold_in(key_of[9], 71), 0),
        "fringe_weight": jnp.clip(0.2 + 0.8 * jax.random.uniform(key_of[8], (DEVICES, DEVICES * CAP), jnp.float32) ** levels(key_of[8], (DEVICES, DEVICES * CAP), ((0, 128),), -0.2, 0.2), 0.2, 1.0),
    }


step_cfl = 0.5

def rotate(block, sign):
    first = block[:, 2 * CELLS:3 * CELLS]
    second = block[:, 3 * CELLS:4 * CELLS]
    cosine = math.cos(2.0 * math.pi / 3.0)
    sine = sign * math.sin(2.0 * math.pi / 3.0)
    return jnp.concatenate([block[:, :2 * CELLS], cosine * first - sine * second, sine * first + cosine * second, block[:, 4 * CELLS:]], axis=1)

def couple(args):
    extended, nbr, coup = args
    near = extended[nbr]
    prod = coup.astype(jnp.float32) * near[:, :, None, :]
    prod = lax.optimization_barrier(jnp.sum(prod, axis=1)).reshape(NB, VARS, VARS, CELLS)
    return lax.optimization_barrier(jnp.sum(prod, axis=2)).reshape(NB, BW)

def precondition(args):
    dinv, resid = args
    prod = (dinv.astype(jnp.float32) * resid[:, None, :]).reshape(NB, VARS, VARS, CELLS)
    return lax.optimization_barrier(jnp.sum(prod, axis=2)).reshape(NB, BW)

def fringe_add(args):
    dst, weight, received = args
    table = (dst[None, :] == jnp.arange(NB, dtype=jnp.int32)[:, None]).astype(jnp.float32) * weight[None, :]
    return jnp.dot(table, received, precision=lax.Precision.HIGHEST)

def operator(psi, source, coupling, neighbours, seam_perm, fringe_src, fringe_dst, fringe_weight):
    grid = psi.reshape(N_BODY, N_BLK, NB, BW)
    lower = jnp.roll(grid[:, :, NB - HB:], 1, axis=1)
    upper = jnp.roll(grid[:, :, :HB], -1, axis=1)
    onehot = (seam_perm[:, :, None] == jnp.arange(HB, dtype=jnp.int32)[None, None, :]).astype(jnp.float32)
    seam_lo = jnp.einsum('bji,bic->bjc', onehot, lower[:, 0], precision=lax.Precision.HIGHEST)
    seam_hi = jnp.einsum('bji,bjc->bic', onehot, upper[:, N_BLK - 1], precision=lax.Precision.HIGHEST)
    seam_lo = rotate(seam_lo.reshape(N_BODY * HB, BW), 1.0).reshape(N_BODY, HB, BW)
    seam_hi = rotate(seam_hi.reshape(N_BODY * HB, BW), -1.0).reshape(N_BODY, HB, BW)
    lower = lower.at[:, 0].set(seam_lo)
    upper = upper.at[:, N_BLK - 1].set(seam_hi)
    extended = jnp.concatenate([lower, grid, upper], axis=2).reshape(DEVICES, NB + 2 * HB, BW)
    coupled = lax.map(couple, (extended, neighbours.reshape(DEVICES, NB, K), coupling.reshape(DEVICES, NB, K, VARS, BW)))
    psi_dev = psi.reshape(DEVICES, NB, BW)
    sent = jnp.take_along_axis(psi_dev, fringe_src[:, :, None], axis=1)
    received = sent.reshape(DEVICES, DEVICES, CAP, BW).transpose(1, 0, 2, 3).reshape(DEVICES, DEVICES * CAP, BW)
    fringe = lax.map(fringe_add, (fringe_dst, fringe_weight, received))
    return source - psi + coupled.reshape(NBT, BW) + fringe.reshape(NBT, BW)

def reference(psi_init, source, coupling, diag_inv, neighbours, seam_perm, fringe_src, fringe_dst, fringe_weight):
    psi = psi_init
    first_norm = None
    resid = psi
    for step in range(STEPS):
        resid = operator(psi, source, coupling, neighbours, seam_perm, fringe_src, fringe_dst, fringe_weight)
        norm_now = jnp.sum(resid * resid) / (NBT * BW) + 1e-06
        if first_norm is None:
            first_norm = norm_now
        cfl = step_cfl * jnp.sqrt(first_norm / norm_now)
        update = lax.map(precondition, (diag_inv.reshape(DEVICES, NB, VARS, BW), resid.reshape(DEVICES, NB, BW)))
        psi = psi + cfl * update.reshape(NBT, BW)
    return (psi, resid)
```

```python
import math

import jax
import jax.numpy as jnp
from jax import lax
from jax.experimental import pallas as pl
from jax.experimental.pallas import tpu as pltpu
from jax.sharding import PartitionSpec as P

CELLS = 64
VARS = 5
BW = 320
NB = 512
SLOTS = 6
RIM = 8
CAP = 8
BODIES = 8
BLKS = 16
DEVS = 128
CHUNKS = 2
CC = CELLS // CHUNKS
CU = VARS * CC
ROWS = CU * CAP // 128
STEPS = 2
CFL = 0.5
LANES = 128
TILES = NB // LANES
TOTAL = DEVS * NB * BW
MESH = pl.DeviceIdType.MESH
F32 = jnp.float32
BF16 = jnp.bfloat16


def iota(shape, dim):
    return lax.broadcasted_iota(jnp.int32, shape, dim)


def split(x):
    hi = x.astype(BF16)
    return hi, (x - hi.astype(F32)).astype(BF16)


def dot(a, b):
    return jnp.dot(a, b, preferred_element_type=F32)


def dot_t(a, b):
    return lax.dot_general(a, b, (((1,), (1,)), ((), ())), preferred_element_type=F32)


def device(o):
    return (lax.div(o, BLKS), lax.rem(o, BLKS))


def kernel(
    psi_hbm, src_hbm, coup_hbm, dinv_hbm, nbr_hbm, perm, fsrc_hbm, fdst_hbm, fw_hbm,
    adj_hbm, res_hbm,
    psi, src, coup, dinv, nbr, fsrc, fdst, fw,
    sel, tab, near_hot, const, rim_hot,
    halves, halo, near, base, fringe, inc_t, prec,
    out, inc, sums, total,
    lsem, ssem, rsem, rim_ssem, rim_rsem, sum_ssem, sum_rsem,
):
    b, k = lax.axis_index("body"), lax.axis_index("blk")
    me = b * BLKS + k
    nxt, prv = lax.rem(k + 1, BLKS), lax.rem(k + BLKS - 1, BLKS)

    loads = [
        pltpu.make_async_copy(s, d, lsem.at[i])
        for i, (s, d) in enumerate(
            [(psi_hbm, psi), (fsrc_hbm, fsrc), (nbr_hbm, nbr), (fdst_hbm, fdst), (fw_hbm, fw),
             (src_hbm, src), (dinv_hbm, dinv), (coup_hbm, coup)]
        )
    ]
    for c in loads:
        c.start()

    bar = pltpu.get_barrier_semaphore()

    def greet(i, carry):
        o = lax.rem(me + i, DEVS)
        pl.semaphore_signal(bar, inc=1, device_id=device(o), device_id_type=MESH)
        return carry

    lax.fori_loop(1, DEVS, greet, 0)

    def slab(ref, s, c, first, count):
        return ref.at[s, c, pl.ds(first, count), pl.ds(0, ROWS)]

    def halve(c):
        for v in range(VARS):
            hi, lo = split(psi[v * CELLS + c * CC : v * CELLS + (c + 1) * CC, :])
            halves[c, 0, v * CC : (v + 1) * CC, :] = hi
            halves[c, 1, v * CC : (v + 1) * CC, :] = lo

    def pack(y):
        n = y.shape[1]
        main = y[:LANES].T.reshape(n // CAP, CAP, LANES)
        rem = y[LANES:]
        parts = [rem] + [pltpu.roll(rem, n - 2 * g, 1) for g in range(1, 4)]
        rest = jnp.concatenate(parts, axis=0).T.reshape(n // CAP, CAP, LANES)
        return main, rest

    def unpack(main, rest):
        n = main.shape[0] * CAP
        top = main.reshape(n, LANES).T
        x = rest.reshape(n, LANES).T
        group = lax.rem(iota((CC, n), 1), CAP) // 2
        low = x[:CC]
        for g in range(1, 4):
            low = jnp.where(group == g, pltpu.roll(x[g * CC : (g + 1) * CC], 2 * g, 1), low)
        return jnp.concatenate([top, low], axis=0)

    def rims(s, c):
        y = dot(halves[c, 0], const[...]) + dot(halves[c, 1], const[...])
        halo[c] = y[:, LANES:]
        main, rest = pack(y[:, :LANES])
        out[s, c, DEVS : DEVS + 2, 0:8] = main[:2]
        out[s, c, DEVS : DEVS + 2, 8:16] = rest[:2]

    def rim_copies(s, c):
        return [
            pltpu.make_async_remote_copy(
                slab(out, s, c, DEVS + i, 1), slab(inc, s, c, DEVS + i, 1),
                rim_ssem.at[s, c, i], rim_rsem.at[s, c, i],
                device_id=(b, to), device_id_type=MESH,
            )
            for i, to in enumerate((nxt, prv))
        ]

    def donors(s, c):
        def block(t, carry):
            cols = pl.ds(pl.multiple_of(t * 256, 256), 256)
            y = dot(halves[c, 0], sel[:, cols]) + dot(halves[c, 1], sel[:, cols])
            main, rest = pack(y)
            out[s, c, pl.ds(t * 32, 32), 0:8] = main
            out[s, c, pl.ds(t * 32, 32), 8:16] = rest
            return carry

        lax.fori_loop(0, 4, block, 0)
        inc[s, c, pl.ds(me, 1)] = out[s, c, pl.ds(me, 1)]

    def send(s, c):
        for r in rim_copies(s, c):
            r.start()

        def one(i, carry):
            o = lax.rem(me + lax.rem(i * 37, DEVS), DEVS)
            pltpu.make_async_remote_copy(
                slab(out, s, c, o, 1), slab(inc, s, c, me, 1), ssem.at[s, c], rsem.at[s, c],
                device_id=device(o), device_id_type=MESH,
            ).start()
            return carry

        lax.fori_loop(1, DEVS, one, 0)

    def wait_rims(s, c):
        for r in rim_copies(s, c):
            r.wait_recv()

    def wait_fringe(s, c):
        ref = slab(inc, s, c, 0, DEVS - 1)
        pltpu.make_async_copy(ref, ref, rsem.at[s, c]).wait()

    def wait_sends(s, c):
        ref = slab(out, s, c, 0, DEVS - 1)
        pltpu.make_async_copy(ref, ref, ssem.at[s, c]).wait()
        for r in rim_copies(s, c):
            r.wait_send()

    def couple(s, c):
        wait_rims(s, c)
        zero = jnp.zeros((14, CAP, LANES), F32)
        main = jnp.concatenate([inc[s, c, DEVS : DEVS + 2, 0:8], zero], axis=0)
        rest = jnp.concatenate([inc[s, c, DEVS : DEVS + 2, 8:16], zero], axis=0)
        hi, lo = split(unpack(main, rest))
        edge = halo[c] + (dot(hi, rim_hot[...]) + dot(lo, rim_hot[...]))
        lane = iota((1, LANES), 1)
        turn_lo = (lane < RIM) & (k == 0)
        turn_hi = (lane >= 56) & (lane < 64) & (k == BLKS - 1)
        cosine = jnp.where(turn_lo | turn_hi, math.cos(2.0 * math.pi / 3.0), 1.0)
        sine = math.sin(2.0 * math.pi / 3.0)
        sine = jnp.where(turn_lo, sine, jnp.where(turn_hi, -sine, 0.0))
        e2, e3 = edge[2 * CC : 3 * CC], edge[3 * CC : 4 * CC]
        edge = jnp.concatenate(
            [edge[: 2 * CC], cosine * e2 - sine * e3, sine * e2 + cosine * e3, edge[4 * CC :]], axis=0
        )
        ehi, elo = split(edge)

        def tile(t, carry):
            cols = pl.ds(pl.multiple_of(t * LANES, LANES), LANES)
            ahi = jnp.concatenate([halves[c, 0, :, cols], ehi], axis=1)
            alo = jnp.concatenate([halves[c, 1, :, cols], elo], axis=1)
            near[...] = dot(ahi, near_hot[t]) + dot(alo, near_hot[t])
            acc = jnp.zeros((VARS, CC, LANES), F32)
            for v in range(VARS):
                rows = slice(v * CELLS + c * CC, v * CELLS + (c + 1) * CC)
                for m in range(SLOTS):
                    x = near[v * CC : (v + 1) * CC, m * LANES : (m + 1) * LANES]
                    acc = acc + coup[m, :, rows, cols].astype(F32) * x[None]
            for v in range(VARS):
                rows = slice(v * CELLS + c * CC, v * CELLS + (c + 1) * CC)
                base[c, v * CC : (v + 1) * CC, cols] = src[rows, cols] - psi[rows, cols] + acc[v]
            return carry

        lax.fori_loop(0, TILES, tile, 0)

    def gather_fringe(s, c):
        wait_fringe(s, c)

        def block(t, carry):
            cols = pl.ds(pl.multiple_of(t * 256, 256), 256)
            x = unpack(inc[s, c, pl.ds(t * 32, 32), 0:8], inc[s, c, pl.ds(t * 32, 32), 8:16])
            hi, lo = split(x * fw[:, cols])
            inc_t[0, :, cols] = hi
            inc_t[1, :, cols] = lo
            return carry

        lax.fori_loop(0, 4, block, 0)
        fringe[...] = dot_t(inc_t[0], tab[...]) + dot_t(inc_t[1], tab[...])

    def residual(s, c, square):
        def tile(t, square):
            cols = pl.ds(pl.multiple_of(t * LANES, LANES), LANES)
            acc = jnp.zeros((VARS, CC, LANES), F32)
            for v in range(VARS):
                rows = slice(v * CELLS + c * CC, v * CELLS + (c + 1) * CC)
                own = slice(v * CC, (v + 1) * CC)
                r = base[c, own, cols] + fringe[own, cols]
                square = square + jnp.sum((r * r).reshape(CC // 8, 8, LANES), axis=0)
                acc = acc + dinv[:, rows, cols].astype(F32) * r[None]
                if s == STEPS - 1:
                    src[rows, cols] = r
            for v in range(VARS):
                rows = slice(v * CELLS + c * CC, v * CELLS + (c + 1) * CC)
                if s == STEPS - 1:
                    prec[rows, cols] = acc[v]
                else:
                    psi[rows, cols] = psi[rows, cols] + CFL * acc[v]
            return square

        return lax.fori_loop(0, TILES, tile, square)

    loads[0].wait()
    loads[1].wait()
    halve(0)
    tgt = iota((1, 2 * LANES), 1)
    h = tgt - LANES
    t, e = h // 16, lax.rem(h, 16)
    own = jnp.where(e < RIM, LANES * t - RIM + e, LANES * (t + 1) + e - RIM)
    own = jnp.where(h < 64, own, -1)
    rim = jnp.where(tgt < RIM, NB - RIM + tgt, jnp.where(tgt < 2 * RIM, tgt - RIM, -1))
    tgt = jnp.where(tgt < LANES, rim, own)

    def build(i, carry):
        at = pl.multiple_of(i * 64, 64)
        row = iota((64, DEVS * CAP), 0) + at
        sel[pl.ds(at, 64)] = jnp.where(row == fsrc[...], 1.0, 0.0).astype(BF16)
        const[pl.ds(at, 64)] = jnp.where(row[:, : 2 * LANES] == tgt, 1.0, 0.0).astype(BF16)
        return carry

    lax.fori_loop(0, NB // 64, build, 0)
    rims(0, 0)
    donors(0, 0)
    pl.semaphore_wait(bar, DEVS - 1)
    send(0, 0)
    for c in range(1, CHUNKS):
        halve(c)
        rims(0, c)
        donors(0, c)
        send(0, c)

    for c in loads[2:5]:
        c.wait()

    def build_in(i, carry):
        at = pl.multiple_of(i * 64, 64)
        row = iota((64, DEVS * CAP), 0) + at
        tab[pl.ds(at, 64)] = jnp.where(row == fdst[...], 1.0, 0.0).astype(BF16)
        return carry

    lax.fori_loop(0, NB // 64, build_in, 0)
    row = iota((2 * LANES, LANES), 0)
    for t in range(TILES):
        for m in range(SLOTS):
            d = nbr[m : m + 1, t * LANES : (t + 1) * LANES] - (RIM + t * LANES)
            d = jnp.where(d < 0, d + (LANES + 16 * t + RIM), jnp.where(d >= LANES, d + (16 * t + RIM), d))
            near_hot[t, :, m * LANES : (m + 1) * LANES] = jnp.where(row == d, 1.0, 0.0).astype(BF16)
    row, col = iota((LANES, LANES), 0), iota((LANES, LANES), 1)
    hot = jnp.zeros((LANES, LANES), F32)
    for j in range(RIM):
        p = perm[0, j]
        low = jnp.where(k == 0, p, j)
        high = jnp.where(k == BLKS - 1, p, j) + 56
        hot = jnp.where((row == low) & (col == j), 1.0, hot)
        hot = jnp.where((row == RIM + j) & (col == high), 1.0, hot)
    rim_hot[...] = hot.astype(BF16)
    for c in loads[5:]:
        c.wait()

    square = [jnp.zeros((8, LANES), F32) for _ in range(STEPS)]
    for s in range(STEPS):
        for c in range(CHUNKS):
            couple(s, c)
        for c in range(CHUNKS):
            gather_fringe(s, c)
            square[s] = residual(s, c, square[s])
            if s < STEPS - 1:
                halve(c)
                rims(s + 1, c)
                donors(s + 1, c)
                send(s + 1, c)

    sums[...] = jnp.concatenate([jnp.sum(x, axis=0, keepdims=True) for x in square], axis=0)[None]
    total[pl.ds(me, 1)] = sums[...]

    def tell(i, carry):
        o = lax.rem(me + i, DEVS)
        pltpu.make_async_remote_copy(
            sums.at[0], total.at[me], sum_ssem, sum_rsem, device_id=device(o), device_id_type=MESH
        ).start()
        return carry

    lax.fori_loop(1, DEVS, tell, 0)
    res = pltpu.make_async_copy(src, res_hbm, lsem.at[0])
    res.start()
    ref = total.at[pl.ds(0, DEVS - 1)]
    pltpu.make_async_copy(ref, ref, sum_rsem).wait()
    q = jnp.sum(jnp.sum(total[...], axis=0), axis=1, keepdims=True) * (1.0 / TOTAL) + 1e-06
    cfl = CFL * jnp.sqrt(q[0:1] / q[1:2])

    def last(i, carry):
        rows = pl.ds(pl.multiple_of(i * 32, 32), 32)
        psi[rows] = psi[rows] + cfl * prec[rows]
        return carry

    lax.fori_loop(0, BW // 32, last, 0)
    adj = pltpu.make_async_copy(psi, adj_hbm, lsem.at[1])
    adj.start()
    pltpu.make_async_copy(ref, ref, sum_ssem).wait()
    for s in range(STEPS):
        for c in range(CHUNKS):
            wait_sends(s, c)
    res.wait()
    adj.wait()


def shards(psi, source, coupling, diag_inv, neighbours, seam_perm, fringe_src, fringe_dst, fringe_weight):
    any_space = pl.BlockSpec(memory_space=pl.ANY)
    vmem = pltpu.VMEM
    dma = pltpu.SemaphoreType.DMA
    slots = DEVS * CAP
    adjoint, residual = pl.pallas_call(
        kernel,
        out_shape=[jax.ShapeDtypeStruct((BW, NB), F32)] * 2,
        in_specs=[any_space] * 5 + [pl.BlockSpec(memory_space=pltpu.SMEM)] + [any_space] * 3,
        out_specs=[any_space] * 2,
        scratch_shapes=[
            vmem((BW, NB), F32),
            vmem((BW, NB), F32),
            vmem((SLOTS, VARS, BW, NB), BF16),
            vmem((VARS, BW, NB), BF16),
            vmem((SLOTS, NB), jnp.int32),
            vmem((1, slots), jnp.int32),
            vmem((1, slots), jnp.int32),
            vmem((1, slots), F32),
            vmem((NB, slots), BF16),
            vmem((NB, slots), BF16),
            vmem((TILES, 2 * LANES, SLOTS * LANES), BF16),
            vmem((NB, 2 * LANES), BF16),
            vmem((LANES, LANES), BF16),
            vmem((CHUNKS, 2, CU, NB), BF16),
            vmem((CHUNKS, CU, LANES), F32),
            vmem((CU, SLOTS * LANES), F32),
            vmem((CHUNKS, CU, NB), F32),
            vmem((CU, NB), F32),
            vmem((2, CU, slots), BF16),
            vmem((BW, NB), F32),
            vmem((STEPS, CHUNKS, DEVS + 2, 16, LANES), F32),
            vmem((STEPS, CHUNKS, DEVS + 2, 16, LANES), F32),
            vmem((1, STEPS, LANES), F32),
            vmem((DEVS, STEPS, LANES), F32),
            dma((8,)),
            dma((STEPS, CHUNKS)),
            dma((STEPS, CHUNKS)),
            dma((STEPS, CHUNKS, 2)),
            dma((STEPS, CHUNKS, 2)),
            dma,
            dma,
        ],
        compiler_params=pltpu.CompilerParams(
            collective_id=0, has_side_effects=True, vmem_limit_bytes=48 << 20
        ),
        name="adjoint_steps",
    )(
        psi.T, source.T, coupling.transpose(1, 2, 3, 0), diag_inv.transpose(1, 2, 0), neighbours.T,
        seam_perm, fringe_src, fringe_dst, fringe_weight,
    )
    return adjoint.T, residual.T


def solution(mesh):
    rows = P(("body", "blk"))
    return jax.shard_map(
        shards,
        mesh=mesh,
        in_specs=(rows, rows, rows, rows, rows, P("body"), rows, rows, rows),
        out_specs=(rows, rows),
        check_vma=False,
    )
```

```python
import math

import jax
import jax.numpy as jnp
from jax import lax
from jax.experimental import pallas as pl
from jax.experimental.pallas import tpu as pltpu
from jax.sharding import PartitionSpec as P

CELLS = 64
VARS = 5
BW = 320
NB = 512
SLOTS = 6
RIM = 8
CAP = 8
GROUPS = 4
GROUP = 32
BODIES = 8
BLKS = 16
DEVS = 128
CHUNKS = 2
CC = CELLS // CHUNKS
CU = VARS * CC
ROWS = CU * CAP // 128
STEPS = 2
CFL = 0.5
LANES = 128
TILES = NB // LANES
TOTAL = DEVS * NB * BW
MESH = pl.DeviceIdType.MESH
F32 = jnp.float32
BF16 = jnp.bfloat16


def iota(shape, dim):
    return lax.broadcasted_iota(jnp.int32, shape, dim)


def split(x):
    hi = x.astype(BF16)
    return jnp.concatenate([hi, (x - hi.astype(F32)).astype(BF16)], axis=0)


def fold(y):
    return y[: y.shape[0] // 2] + y[y.shape[0] // 2 :]


def dot(a, b):
    return fold(jnp.dot(a, b, preferred_element_type=F32))


def dot_t(a, b):
    return fold(lax.dot_general(a, b, (((1,), (1,)), ((), ())), preferred_element_type=F32))


def device(o):
    return (lax.div(o, BLKS), lax.rem(o, BLKS))


def kernel(
    psi_hbm, src_hbm, coup_hbm, dinv_hbm, nbr_hbm, perm_hbm, fsrc_hbm, fdst_hbm, fw_hbm,
    adj_hbm, res_hbm,
    psi, src, coup, dinv, nbr, perm, fsrc, fdst, fw,
    sel, tab, near_hot, const, rim_hot,
    halves, halo, near, base, fringe, prec,
    out, inc, sums, total,
    lsem, ssem, rsem, rim_ssem, rim_rsem, sum_ssem, sum_rsem,
):
    b, k = lax.axis_index("body"), lax.axis_index("blk")
    me = b * BLKS + k
    group = lax.div(me, GROUP)
    nxt, prv = lax.rem(k + 1, BLKS), lax.rem(k + BLKS - 1, BLKS)

    loads = [
        pltpu.make_async_copy(s, d, lsem.at[i])
        for i, (s, d) in enumerate(
            [(psi_hbm, psi), (fsrc_hbm, fsrc), (nbr_hbm, nbr), (perm_hbm, perm), (fdst_hbm, fdst), (fw_hbm, fw),
             (src_hbm, src), (dinv_hbm, dinv), (coup_hbm, coup)]
        )
    ]
    for c in loads:
        c.start()

    bar = pltpu.get_barrier_semaphore()

    def greet(i, carry):
        o = lax.rem(me + i, DEVS)
        pl.semaphore_signal(bar, inc=1, device_id=device(o), device_id_type=MESH)
        return carry

    lax.fori_loop(1, DEVS, greet, 0)

    def slab(ref, s, c, first, count):
        return ref.at[s, c, pl.ds(first, count), pl.ds(0, ROWS)]

    def halve(c):
        for v in range(VARS):
            both = split(psi[v * CELLS + c * CC : v * CELLS + (c + 1) * CC, :])
            halves[c, v * CC : (v + 1) * CC, :] = both[:CC]
            halves[c, CU + v * CC : CU + (v + 1) * CC, :] = both[CC:]

    def pack(y):
        n = y.shape[1]
        main = y[:LANES].T.reshape(n // CAP, CAP, LANES)
        rem = y[LANES:]
        parts = [rem] + [pltpu.roll(rem, n - 2 * g, 1) for g in range(1, 4)]
        rest = jnp.concatenate(parts, axis=0).T.reshape(n // CAP, CAP, LANES)
        return main, rest

    def unpack(main, rest):
        n = main.shape[0] * CAP
        top = main.reshape(n, LANES).T
        x = rest.reshape(n, LANES).T
        group = lax.rem(iota((CC, n), 1), CAP) // 2
        low = x[:CC]
        for g in range(1, 4):
            low = jnp.where(group == g, pltpu.roll(x[g * CC : (g + 1) * CC], 2 * g, 1), low)
        return jnp.concatenate([top, low], axis=0)

    def rims(s, c):
        y = dot(halves[c], const[...])
        halo[c] = y[:, LANES:]
        main, rest = pack(y[:, :LANES])
        out[s, c, DEVS : DEVS + 2, 0:8] = main[:2]
        out[s, c, DEVS : DEVS + 2, 8:16] = rest[:2]

    def rim_copies(s, c):
        return [
            pltpu.make_async_remote_copy(
                slab(out, s, c, DEVS + i, 1), slab(inc, s, c, DEVS + i, 1),
                rim_ssem.at[s, c, i], rim_rsem.at[s, c, i],
                device_id=(b, to), device_id_type=MESH,
            )
            for i, to in enumerate((nxt, prv))
        ]

    def donors(s, c):
        def block(t, carry):
            cols = pl.ds(pl.multiple_of(t * 256, 256), 256)
            y = dot(halves[c], sel[:, cols])
            main, rest = pack(y)
            out[s, c, pl.ds(t * 32, 32), 0:8] = main
            out[s, c, pl.ds(t * 32, 32), 8:16] = rest
            return carry

        lax.fori_loop(0, 4, block, 0)
        inc[s, c, pl.ds(me, 1)] = out[s, c, pl.ds(me, 1)]

    def send_rims(s, c):
        for r in rim_copies(s, c):
            r.start()

    def send_to(s, c, i):
        o = lax.rem(me + i, DEVS)
        pltpu.make_async_remote_copy(
            slab(out, s, c, o, 1), slab(inc, s, c, me, 1), ssem.at[s, c], rsem.at[s, c, group],
            device_id=device(o), device_id_type=MESH,
        ).start()

    def send(s, c):
        def one(i, carry):
            send_to(s, c, i)
            return carry

        lax.fori_loop(1, DEVS, one, 0)

    def wait_rims(s, c):
        for r in rim_copies(s, c):
            r.wait_recv()

    def wait_group(s, c, g, count):
        ref = slab(inc, s, c, 0, count)
        pltpu.make_async_copy(ref, ref, rsem.at[s, c, g]).wait()

    def wait_sends(s, c):
        ref = slab(out, s, c, 0, DEVS - 1)
        pltpu.make_async_copy(ref, ref, ssem.at[s, c]).wait()
        for r in rim_copies(s, c):
            r.wait_send()

    def couple(s, c, sends=None):
        wait_rims(s, c)
        zero = jnp.zeros((14, CAP, LANES), F32)
        main = jnp.concatenate([inc[s, c, DEVS : DEVS + 2, 0:8], zero], axis=0)
        rest = jnp.concatenate([inc[s, c, DEVS : DEVS + 2, 8:16], zero], axis=0)
        edge = halo[c] + dot(split(unpack(main, rest)), rim_hot[...])
        lane = iota((1, LANES), 1)
        turn_lo = (lane < RIM) & (k == 0)
        turn_hi = (lane >= 56) & (lane < 64) & (k == BLKS - 1)
        cosine = jnp.where(turn_lo | turn_hi, math.cos(2.0 * math.pi / 3.0), 1.0)
        sine = math.sin(2.0 * math.pi / 3.0)
        sine = jnp.where(turn_lo, sine, jnp.where(turn_hi, -sine, 0.0))
        e2, e3 = edge[2 * CC : 3 * CC], edge[3 * CC : 4 * CC]
        edge = jnp.concatenate(
            [edge[: 2 * CC], cosine * e2 - sine * e3, sine * e2 + cosine * e3, edge[4 * CC :]], axis=0
        )
        edge = split(edge)

        def tile(t, carry):
            cols = pl.ds(pl.multiple_of(t * LANES, LANES), LANES)
            near[...] = dot(jnp.concatenate([halves[c, :, cols], edge], axis=1), near_hot[t])
            if sends:
                send_to(*sends, t * GROUP + 1)
            acc = jnp.zeros((VARS, CC, LANES), F32)
            for v in range(VARS):
                rows = slice(v * CELLS + c * CC, v * CELLS + (c + 1) * CC)
                for m in range(SLOTS):
                    if sends:
                        send_to(*sends, t * GROUP + 2 + v * SLOTS + m)
                    x = near[v * CC : (v + 1) * CC, m * LANES : (m + 1) * LANES]
                    acc = acc + coup[m, :, rows, cols].astype(F32) * x[None]
            for v in range(VARS):
                rows = slice(v * CELLS + c * CC, v * CELLS + (c + 1) * CC)
                base[c, v * CC : (v + 1) * CC, cols] = src[rows, cols] - psi[rows, cols] + acc[v]
            if sends:

                @pl.when(t < TILES - 1)
                def _():
                    send_to(*sends, t * GROUP + GROUP)

            return carry

        lax.fori_loop(0, TILES, tile, 0)

    def gather_fringe(s, c):
        def block(g):
            cols = pl.ds(pl.multiple_of(g * 256, 256), 256)
            x = unpack(inc[s, c, pl.ds(g * GROUP, GROUP), 0:8], inc[s, c, pl.ds(g * GROUP, GROUP), 8:16])
            return dot_t(split(x * fw[:, cols]), tab[:, cols])

        fringe[...] = jnp.zeros_like(fringe)

        def other(i, carry):
            g = lax.rem(group + GROUPS - i, GROUPS)
            wait_group(s, c, g, GROUP)
            fringe[...] += block(g)
            return carry

        lax.fori_loop(1, GROUPS, other, 0)
        wait_group(s, c, group, GROUP - 1)
        fringe[...] += block(group)

    def residual(s, c, square):
        def tile(t, square):
            cols = pl.ds(pl.multiple_of(t * LANES, LANES), LANES)
            acc = jnp.zeros((VARS, CC, LANES), F32)
            for v in range(VARS):
                rows = slice(v * CELLS + c * CC, v * CELLS + (c + 1) * CC)
                own = slice(v * CC, (v + 1) * CC)
                r = base[c, own, cols] + fringe[own, cols]
                square = square + jnp.sum((r * r).reshape(CC // 8, 8, LANES), axis=0)
                if s == STEPS - 1:
                    src[rows, cols] = r
                else:
                    acc = acc + dinv[:, rows, cols].astype(F32) * r[None]
            if s < STEPS - 1:
                for v in range(VARS):
                    rows = slice(v * CELLS + c * CC, v * CELLS + (c + 1) * CC)
                    psi[rows, cols] = psi[rows, cols] + CFL * acc[v]
            return square

        return lax.fori_loop(0, TILES, tile, square)

    loads[0].wait()
    loads[1].wait()
    halve(0)
    tgt = iota((1, 2 * LANES), 1)
    h = tgt - LANES
    t, e = h // 16, lax.rem(h, 16)
    own = jnp.where(e < RIM, LANES * t - RIM + e, LANES * (t + 1) + e - RIM)
    own = jnp.where(h < 64, own, -1)
    rim = jnp.where(tgt < RIM, NB - RIM + tgt, jnp.where(tgt < 2 * RIM, tgt - RIM, -1))
    tgt = jnp.where(tgt < LANES, rim, own)

    def build(i, carry):
        at = pl.multiple_of(i * 64, 64)
        row = iota((64, DEVS * CAP), 0) + at
        sel[pl.ds(at, 64)] = jnp.where(row == fsrc[...], 1.0, 0.0).astype(BF16)
        const[pl.ds(at, 64)] = jnp.where(row[:, : 2 * LANES] == tgt, 1.0, 0.0).astype(BF16)
        return carry

    lax.fori_loop(0, NB // 64, build, 0)
    rims(0, 0)
    donors(0, 0)
    pl.semaphore_wait(bar, DEVS - 1)
    send_rims(0, 0)
    send(0, 0)
    halve(1)
    rims(0, 1)
    send_rims(0, 1)
    donors(0, 1)

    for c in loads[2:6]:
        c.wait()

    def build_in(i, carry):
        at = pl.multiple_of(i * 64, 64)
        row = iota((64, DEVS * CAP), 0) + at
        tab[pl.ds(at, 64)] = jnp.where(row == fdst[...], 1.0, 0.0).astype(BF16)
        return carry

    lax.fori_loop(0, NB // 64, build_in, 0)
    row = iota((2 * LANES, LANES), 0)
    for t in range(TILES):
        for m in range(SLOTS):
            d = nbr[m : m + 1, t * LANES : (t + 1) * LANES] - (RIM + t * LANES)
            d = jnp.where(d < 0, d + (LANES + 16 * t + RIM), jnp.where(d >= LANES, d + (16 * t + RIM), d))
            near_hot[t, :, m * LANES : (m + 1) * LANES] = jnp.where(row == d, 1.0, 0.0).astype(BF16)
    row, col = iota((LANES, LANES), 0), iota((LANES, LANES), 1)
    hot = jnp.zeros((LANES, LANES), F32)
    for j in range(RIM):
        p = perm[0, j]
        low = jnp.where(k == 0, p, j)
        high = jnp.where(k == BLKS - 1, p, j) + 56
        hot = jnp.where((row == low) & (col == j), 1.0, hot)
        hot = jnp.where((row == RIM + j) & (col == high), 1.0, hot)
    rim_hot[...] = hot.astype(BF16)
    for c in loads[6:]:
        c.wait()

    square = [jnp.zeros((8, LANES), F32) for _ in range(STEPS)]
    order = [(s, c) for s in range(STEPS) for c in range(CHUNKS)]
    pending = (0, 1)
    for s, c in order:
        couple(s, c, pending)
        pending = None
        gather_fringe(s, c)
        square[s] = residual(s, c, square[s])
        if s < STEPS - 1:
            halve(c)
            rims(s + 1, c)
            send_rims(s + 1, c)
            donors(s + 1, c)
            pending = (s + 1, c)

    sums[...] = jnp.concatenate([jnp.sum(x, axis=0, keepdims=True) for x in square], axis=0)[None]
    total[pl.ds(me, 1)] = sums[...]

    def tell(i, carry):
        o = lax.rem(me + i, DEVS)
        pltpu.make_async_remote_copy(
            sums.at[0], total.at[me], sum_ssem, sum_rsem, device_id=device(o), device_id_type=MESH
        ).start()
        return carry

    lax.fori_loop(1, DEVS, tell, 0)
    res = pltpu.make_async_copy(src, res_hbm, lsem.at[0])
    res.start()

    def precondition(i, carry):
        c, t = lax.div(i, TILES), lax.rem(i, TILES)
        cols = pl.ds(pl.multiple_of(t * LANES, LANES), LANES)
        acc = jnp.zeros((VARS, CC, LANES), F32)
        for v in range(VARS):
            rows = pl.ds(pl.multiple_of(v * CELLS + c * CC, CC), CC)
            acc = acc + dinv[:, rows, cols].astype(F32) * src[rows, cols][None]
        for v in range(VARS):
            prec[pl.ds(pl.multiple_of(v * CELLS + c * CC, CC), CC), cols] = acc[v]
        return carry

    lax.fori_loop(0, CHUNKS * TILES, precondition, 0)
    ref = total.at[pl.ds(0, DEVS - 1)]
    pltpu.make_async_copy(ref, ref, sum_rsem).wait()
    q = jnp.sum(jnp.sum(total[...], axis=0), axis=1, keepdims=True) * (1.0 / TOTAL) + 1e-06
    cfl = CFL * jnp.sqrt(q[0:1] / q[1:2])

    def last(i, carry):
        rows = pl.ds(pl.multiple_of(i * 32, 32), 32)
        psi[rows] = psi[rows] + cfl * prec[rows]
        return carry

    lax.fori_loop(0, BW // 32, last, 0)
    adj = pltpu.make_async_copy(psi, adj_hbm, lsem.at[1])
    adj.start()
    pltpu.make_async_copy(ref, ref, sum_ssem).wait()
    for s in range(STEPS):
        for c in range(CHUNKS):
            wait_sends(s, c)
    res.wait()
    adj.wait()


def shards(psi, source, coupling, diag_inv, neighbours, seam_perm, fringe_src, fringe_dst, fringe_weight):
    any_space = pl.BlockSpec(memory_space=pl.ANY)
    vmem = pltpu.VMEM
    dma = pltpu.SemaphoreType.DMA
    slots = DEVS * CAP
    adjoint, residual = pl.pallas_call(
        kernel,
        out_shape=[jax.ShapeDtypeStruct((BW, NB), F32)] * 2,
        in_specs=[any_space] * 9,
        out_specs=[any_space] * 2,
        scratch_shapes=[
            vmem((BW, NB), F32),
            vmem((BW, NB), F32),
            vmem((SLOTS, VARS, BW, NB), BF16),
            vmem((VARS, BW, NB), BF16),
            vmem((SLOTS, NB), jnp.int32),
            pltpu.SMEM((1, RIM), jnp.int32),
            vmem((1, slots), jnp.int32),
            vmem((1, slots), jnp.int32),
            vmem((1, slots), F32),
            vmem((NB, slots), BF16),
            vmem((NB, slots), BF16),
            vmem((TILES, 2 * LANES, SLOTS * LANES), BF16),
            vmem((NB, 2 * LANES), BF16),
            vmem((LANES, LANES), BF16),
            vmem((CHUNKS, 2 * CU, NB), BF16),
            vmem((CHUNKS, CU, LANES), F32),
            vmem((CU, SLOTS * LANES), F32),
            vmem((CHUNKS, CU, NB), F32),
            vmem((CU, NB), F32),
            vmem((BW, NB), F32),
            vmem((STEPS, CHUNKS, DEVS + 2, 16, LANES), F32),
            vmem((STEPS, CHUNKS, DEVS + 2, 16, LANES), F32),
            vmem((1, STEPS, LANES), F32),
            vmem((DEVS, STEPS, LANES), F32),
            dma((9,)),
            dma((STEPS, CHUNKS)),
            dma((STEPS, CHUNKS, GROUPS)),
            dma((STEPS, CHUNKS, 2)),
            dma((STEPS, CHUNKS, 2)),
            dma,
            dma,
        ],
        compiler_params=pltpu.CompilerParams(
            collective_id=0, has_side_effects=True, vmem_limit_bytes=40 << 20
        ),
        name="adjoint_steps",
    )(
        *[pltpu.with_memory_space_constraint(x, pltpu.HBM) for x in (psi.T, source.T, coupling.transpose(1, 2, 3, 0), diag_inv.transpose(1, 2, 0), neighbours.T,
        seam_perm, fringe_src, fringe_dst, fringe_weight)]
    )
    return adjoint.T, residual.T


def solution(mesh):
    rows = P(("body", "blk"))
    return jax.shard_map(
        shards,
        mesh=mesh,
        in_specs=(rows, rows, rows, rows, rows, P("body"), rows, rows, rows),
        out_specs=(rows, rows),
        check_vma=False,
    )
```

```python
import math

import jax
import jax.numpy as jnp
from jax import lax
from jax.experimental import pallas as pl
from jax.experimental.pallas import tpu as pltpu
from jax.sharding import PartitionSpec as P

CELLS = 64
VARS = 5
BW = 320
NB = 512
SLOTS = 6
RIM = 8
CAP = 8
GROUPS = 4
GROUP = 32
BODIES = 8
BLKS = 16
DEVS = 128
CHUNKS = 2
CC = CELLS // CHUNKS
CU = VARS * CC
ROWS = CU * CAP // 128
STEPS = 2
CFL = 0.5
LANES = 128
TILES = NB // LANES
TOTAL = DEVS * NB * BW
MESH = pl.DeviceIdType.MESH
F32 = jnp.float32
BF16 = jnp.bfloat16


def iota(shape, dim):
    return lax.broadcasted_iota(jnp.int32, shape, dim)


def split(x):
    hi = x.astype(BF16)
    return jnp.concatenate([hi, (x - hi.astype(F32)).astype(BF16)], axis=0)


def fold(y):
    return y[: y.shape[0] // 2] + y[y.shape[0] // 2 :]


def dot(a, b):
    return fold(jnp.dot(a, b, preferred_element_type=F32))


def dot_t(a, b):
    return fold(lax.dot_general(a, b, (((1,), (1,)), ((), ())), preferred_element_type=F32))


def device(o):
    return (lax.div(o, BLKS), lax.rem(o, BLKS))


def far_first(b, k):
    y, core, z, x = lax.div(b, 2), lax.rem(b, 2), lax.div(k, 4), lax.rem(k, 4)
    bodies = {(i, j): lax.rem(y + i, 4) * 2 + lax.rem(core + j, 2) for i in range(4) for j in range(2)}
    blks = {(i, j): lax.rem(z + i, 4) * 4 + lax.rem(x + j, 4) for i in range(4) for j in range(4)}
    steps = [(p, q) for p in bodies for q in blks if any(p + q)]
    hops = (0, 1, 2, 1)
    steps.sort(key=lambda s: -(hops[s[0][0]] + hops[s[1][0]] + hops[s[1][1]]))
    return [(bodies[p], blks[q]) for p, q in steps]


def kernel(
    psi_hbm, src_hbm, coup_hbm, dinv_hbm, nbr_hbm, perm_hbm, fsrc_hbm, fdst_hbm, fw_hbm,
    results,
    psi, src, coup, dinv, nbr, perm, fsrc, fdst, fw,
    sel, tab, near_hot, const, rim_hot,
    halves, halo, near, base, fringe, prec,
    out, inc, sums, total,
    lsem, ssem, rsem, rim_ssem, rim_rsem, sum_ssem, sum_rsem, row_sem,
):
    b, k = lax.axis_index("body"), lax.axis_index("blk")
    me = b * BLKS + k
    adj, res = results.at[0], results.at[1]
    group = lax.div(me, GROUP)
    nxt, prv = lax.rem(k + 1, BLKS), lax.rem(k + BLKS - 1, BLKS)

    loads = [
        pltpu.make_async_copy(s, d, lsem.at[i])
        for i, (s, d) in enumerate(
            [(psi_hbm, psi), (fsrc_hbm, fsrc), (nbr_hbm, nbr), (perm_hbm, perm), (fdst_hbm, fdst), (fw_hbm, fw),
             (src_hbm, src), (dinv_hbm, dinv), (coup_hbm, coup)]
        )
    ]
    for c in loads:
        c.start()

    bar = pltpu.get_barrier_semaphore()

    def greet_row(i, carry):
        pl.semaphore_signal(bar, inc=1, device_id=(b, lax.rem(k + i, BLKS)), device_id_type=MESH)
        return carry

    def tell_column(sem):
        def one(i, carry):
            pl.semaphore_signal(sem, inc=1, device_id=(lax.rem(b + i, BODIES), k), device_id_type=MESH)
            return carry

        lax.fori_loop(1, BODIES, one, 0)

    lax.fori_loop(1, BLKS, greet_row, 0)
    tell_column(bar)

    def slab(ref, s, c, first, count):
        return ref.at[s, c, pl.ds(first, count), pl.ds(0, ROWS)]

    def halve(c):
        for v in range(VARS):
            both = split(psi[v * CELLS + c * CC : v * CELLS + (c + 1) * CC, :])
            halves[c, v * CC : (v + 1) * CC, :] = both[:CC]
            halves[c, CU + v * CC : CU + (v + 1) * CC, :] = both[CC:]

    def pack(y):
        n = y.shape[1]
        main = y[:LANES].T.reshape(n // CAP, CAP, LANES)
        rem = y[LANES:]
        parts = [rem] + [pltpu.roll(rem, n - 2 * g, 1) for g in range(1, 4)]
        rest = jnp.concatenate(parts, axis=0).T.reshape(n // CAP, CAP, LANES)
        return main, rest

    def unpack(main, rest):
        n = main.shape[0] * CAP
        top = main.reshape(n, LANES).T
        x = rest.reshape(n, LANES).T
        group = lax.rem(iota((CC, n), 1), CAP) // 2
        low = x[:CC]
        for g in range(1, 4):
            low = jnp.where(group == g, pltpu.roll(x[g * CC : (g + 1) * CC], 2 * g, 1), low)
        return jnp.concatenate([top, low], axis=0)

    def rims(s, c):
        y = dot(halves[c], const[...])
        halo[c] = y[:, LANES:]
        main, rest = pack(y[:, :LANES])
        out[s, c, DEVS : DEVS + 2, 0:8] = main[:2]
        out[s, c, DEVS : DEVS + 2, 8:16] = rest[:2]

    def rim_copies(s, c):
        return [
            pltpu.make_async_remote_copy(
                slab(out, s, c, DEVS + i, 1), slab(inc, s, c, DEVS + i, 1),
                rim_ssem.at[s, c, i], rim_rsem.at[s, c, i],
                device_id=(b, to), device_id_type=MESH,
            )
            for i, to in enumerate((nxt, prv))
        ]

    def donors(s, c):
        def block(t, carry):
            cols = pl.ds(pl.multiple_of(t * 256, 256), 256)
            y = dot(halves[c], sel[:, cols])
            main, rest = pack(y)
            out[s, c, pl.ds(t * 32, 32), 0:8] = main
            out[s, c, pl.ds(t * 32, 32), 8:16] = rest
            return carry

        lax.fori_loop(0, 4, block, 0)
        inc[s, c, pl.ds(me, 1)] = out[s, c, pl.ds(me, 1)]

    def send_rims(s, c):
        for r in rim_copies(s, c):
            r.start()

    def send_to(s, c, i):
        o = lax.rem(me + i, DEVS)
        pltpu.make_async_remote_copy(
            slab(out, s, c, o, 1), slab(inc, s, c, me, 1), ssem.at[s, c], rsem.at[s, c, group],
            device_id=device(o), device_id_type=MESH,
        ).start()

    def send(s, c):
        def one(i, carry):
            send_to(s, c, i)
            return carry

        lax.fori_loop(1, DEVS, one, 0)

    def wait_rims(s, c):
        for r in rim_copies(s, c):
            r.wait_recv()

    def wait_group(s, c, g, count):
        ref = slab(inc, s, c, 0, count)
        pltpu.make_async_copy(ref, ref, rsem.at[s, c, g]).wait()

    def wait_sends(s, c):
        ref = slab(out, s, c, 0, DEVS - 1)
        pltpu.make_async_copy(ref, ref, ssem.at[s, c]).wait()
        for r in rim_copies(s, c):
            r.wait_send()

    def couple(s, c, sends=None):
        wait_rims(s, c)
        zero = jnp.zeros((14, CAP, LANES), F32)
        main = jnp.concatenate([inc[s, c, DEVS : DEVS + 2, 0:8], zero], axis=0)
        rest = jnp.concatenate([inc[s, c, DEVS : DEVS + 2, 8:16], zero], axis=0)
        edge = halo[c] + dot(split(unpack(main, rest)), rim_hot[...])
        lane = iota((1, LANES), 1)
        turn_lo = (lane < RIM) & (k == 0)
        turn_hi = (lane >= 56) & (lane < 64) & (k == BLKS - 1)
        cosine = jnp.where(turn_lo | turn_hi, math.cos(2.0 * math.pi / 3.0), 1.0)
        sine = math.sin(2.0 * math.pi / 3.0)
        sine = jnp.where(turn_lo, sine, jnp.where(turn_hi, -sine, 0.0))
        e2, e3 = edge[2 * CC : 3 * CC], edge[3 * CC : 4 * CC]
        edge = jnp.concatenate(
            [edge[: 2 * CC], cosine * e2 - sine * e3, sine * e2 + cosine * e3, edge[4 * CC :]], axis=0
        )
        edge = split(edge)

        def tile(t, carry):
            cols = pl.ds(pl.multiple_of(t * LANES, LANES), LANES)
            near[...] = dot(jnp.concatenate([halves[c, :, cols], edge], axis=1), near_hot[t])
            if sends:
                send_to(*sends, t * GROUP + 1)
            acc = jnp.zeros((VARS, CC, LANES), F32)
            for v in range(VARS):
                rows = slice(v * CELLS + c * CC, v * CELLS + (c + 1) * CC)
                for m in range(SLOTS):
                    if sends:
                        send_to(*sends, t * GROUP + 2 + v * SLOTS + m)
                    x = near[v * CC : (v + 1) * CC, m * LANES : (m + 1) * LANES]
                    acc = acc + coup[m, :, rows, cols].astype(F32) * x[None]
            for v in range(VARS):
                rows = slice(v * CELLS + c * CC, v * CELLS + (c + 1) * CC)
                base[c, v * CC : (v + 1) * CC, cols] = src[rows, cols] - psi[rows, cols] + acc[v]
            if sends:

                @pl.when(t < TILES - 1)
                def _():
                    send_to(*sends, t * GROUP + GROUP)

            return carry

        lax.fori_loop(0, TILES, tile, 0)

    def gather_fringe(s, c):
        def block(g):
            cols = pl.ds(pl.multiple_of(g * 256, 256), 256)
            x = unpack(inc[s, c, pl.ds(g * GROUP, GROUP), 0:8], inc[s, c, pl.ds(g * GROUP, GROUP), 8:16])
            return dot_t(split(x * fw[:, cols]), tab[:, cols])

        fringe[...] = jnp.zeros_like(fringe)

        def other(i, carry):
            g = lax.rem(group + GROUPS - i, GROUPS)
            wait_group(s, c, g, GROUP)
            fringe[...] += block(g)
            return carry

        lax.fori_loop(1, GROUPS, other, 0)
        wait_group(s, c, group, GROUP - 1)
        fringe[...] += block(group)

    def residual(s, c, square):
        def tile(t, square):
            cols = pl.ds(pl.multiple_of(t * LANES, LANES), LANES)
            acc = jnp.zeros((VARS, CC, LANES), F32)
            for v in range(VARS):
                rows = slice(v * CELLS + c * CC, v * CELLS + (c + 1) * CC)
                own = slice(v * CC, (v + 1) * CC)
                r = base[c, own, cols] + fringe[own, cols]
                square = square + jnp.sum((r * r).reshape(CC // 8, 8, LANES), axis=0)
                if s == STEPS - 1:
                    res[rows, cols] = r
                else:
                    acc = acc + dinv[:, rows, cols].astype(F32) * r[None]
            if s < STEPS - 1:
                for v in range(VARS):
                    rows = slice(v * CELLS + c * CC, v * CELLS + (c + 1) * CC)
                    psi[rows, cols] = psi[rows, cols] + CFL * acc[v]
            return square

        return lax.fori_loop(0, TILES, tile, square)

    loads[0].wait()
    loads[1].wait()
    halve(0)
    tgt = iota((1, 2 * LANES), 1)
    h = tgt - LANES
    t, e = h // 16, lax.rem(h, 16)
    own = jnp.where(e < RIM, LANES * t - RIM + e, LANES * (t + 1) + e - RIM)
    own = jnp.where(h < 64, own, -1)
    rim = jnp.where(tgt < RIM, NB - RIM + tgt, jnp.where(tgt < 2 * RIM, tgt - RIM, -1))
    tgt = jnp.where(tgt < LANES, rim, own)

    def build(i, carry):
        at = pl.multiple_of(i * 64, 64)
        row = iota((64, DEVS * CAP), 0) + at
        sel[pl.ds(at, 64)] = jnp.where(row == fsrc[...], 1.0, 0.0).astype(BF16)
        const[pl.ds(at, 64)] = jnp.where(row[:, : 2 * LANES] == tgt, 1.0, 0.0).astype(BF16)
        return carry

    lax.fori_loop(0, NB // 64, build, 0)
    pl.semaphore_wait(bar, BLKS - 1 + BODIES - 1)
    tell_column(row_sem)
    rims(0, 0)
    donors(0, 0)
    pl.semaphore_wait(row_sem, BODIES - 1)
    send_rims(0, 0)
    send(0, 0)
    halve(1)
    rims(0, 1)
    send_rims(0, 1)
    donors(0, 1)

    for c in loads[2:6]:
        c.wait()

    def build_in(i, carry):
        at = pl.multiple_of(i * 64, 64)
        row = iota((64, DEVS * CAP), 0) + at
        tab[pl.ds(at, 64)] = jnp.where(row == fdst[...], 1.0, 0.0).astype(BF16)
        return carry

    lax.fori_loop(0, NB // 64, build_in, 0)
    row = iota((2 * LANES, LANES), 0)
    for t in range(TILES):
        for m in range(SLOTS):
            d = nbr[m : m + 1, t * LANES : (t + 1) * LANES] - (RIM + t * LANES)
            d = jnp.where(d < 0, d + (LANES + 16 * t + RIM), jnp.where(d >= LANES, d + (16 * t + RIM), d))
            near_hot[t, :, m * LANES : (m + 1) * LANES] = jnp.where(row == d, 1.0, 0.0).astype(BF16)
    row, col = iota((LANES, LANES), 0), iota((LANES, LANES), 1)
    hot = jnp.zeros((LANES, LANES), F32)
    for j in range(RIM):
        p = perm[0, j]
        low = jnp.where(k == 0, p, j)
        high = jnp.where(k == BLKS - 1, p, j) + 56
        hot = jnp.where((row == low) & (col == j), 1.0, hot)
        hot = jnp.where((row == RIM + j) & (col == high), 1.0, hot)
    rim_hot[...] = hot.astype(BF16)
    for c in loads[6:]:
        c.wait()

    square = [jnp.zeros((8, LANES), F32) for _ in range(STEPS)]
    order = [(s, c) for s in range(STEPS) for c in range(CHUNKS)]
    pending = (0, 1)
    for s, c in order:
        couple(s, c, pending)
        pending = None
        gather_fringe(s, c)
        square[s] = residual(s, c, square[s])
        if s < STEPS - 1:
            halve(c)
            rims(s + 1, c)
            send_rims(s + 1, c)
            donors(s + 1, c)
            pending = (s + 1, c)

    sums[...] = jnp.concatenate([jnp.sum(x, axis=0, keepdims=True) for x in square], axis=0)[None]
    total[pl.ds(me, 1)] = sums[...]

    for to in far_first(b, k):
        pltpu.make_async_remote_copy(
            sums.at[0], total.at[me], sum_ssem, sum_rsem, device_id=to, device_id_type=MESH
        ).start()

    def precondition(i, carry):
        c, t = lax.div(i, TILES), lax.rem(i, TILES)
        cols = pl.ds(pl.multiple_of(t * LANES, LANES), LANES)
        acc = jnp.zeros((VARS, CC, LANES), F32)
        for v in range(VARS):
            rows = pl.ds(pl.multiple_of(v * CELLS + c * CC, CC), CC)
            acc = acc + dinv[:, rows, cols].astype(F32) * res[rows, cols][None]
        for v in range(VARS):
            prec[pl.ds(pl.multiple_of(v * CELLS + c * CC, CC), CC), cols] = acc[v]
        return carry

    lax.fori_loop(0, CHUNKS * TILES, precondition, 0)
    ref = total.at[pl.ds(0, DEVS - 1)]
    pltpu.make_async_copy(ref, ref, sum_rsem).wait()
    q = jnp.sum(jnp.sum(total[...], axis=0), axis=1, keepdims=True) * (1.0 / TOTAL) + 1e-06
    cfl = CFL * jnp.sqrt(q[0:1] / q[1:2])

    def last(i, carry):
        rows = pl.ds(pl.multiple_of(i * 32, 32), 32)
        adj[rows] = psi[rows] + cfl * prec[rows]
        return carry

    lax.fori_loop(0, BW // 32, last, 0)
    pltpu.make_async_copy(ref, ref, sum_ssem).wait()
    for s in range(STEPS):
        for c in range(CHUNKS):
            wait_sends(s, c)


def shards(psi, source, coupling, diag_inv, neighbours, seam_perm, fringe_src, fringe_dst, fringe_weight):
    any_space = pl.BlockSpec(memory_space=pl.ANY)
    vmem = pltpu.VMEM
    dma = pltpu.SemaphoreType.DMA
    slots = DEVS * CAP
    results = pl.pallas_call(
        kernel,
        out_shape=jax.ShapeDtypeStruct((2, BW, NB), F32),
        in_specs=[any_space] * 9,
        out_specs=pl.BlockSpec(memory_space=vmem),
        scratch_shapes=[
            vmem((BW, NB), F32),
            vmem((BW, NB), F32),
            vmem((SLOTS, VARS, BW, NB), BF16),
            vmem((VARS, BW, NB), BF16),
            vmem((SLOTS, NB), jnp.int32),
            pltpu.SMEM((1, RIM), jnp.int32),
            vmem((1, slots), jnp.int32),
            vmem((1, slots), jnp.int32),
            vmem((1, slots), F32),
            vmem((NB, slots), BF16),
            vmem((NB, slots), BF16),
            vmem((TILES, 2 * LANES, SLOTS * LANES), BF16),
            vmem((NB, 2 * LANES), BF16),
            vmem((LANES, LANES), BF16),
            vmem((CHUNKS, 2 * CU, NB), BF16),
            vmem((CHUNKS, CU, LANES), F32),
            vmem((CU, SLOTS * LANES), F32),
            vmem((CHUNKS, CU, NB), F32),
            vmem((CU, NB), F32),
            vmem((BW, NB), F32),
            vmem((STEPS, CHUNKS, DEVS + 2, 16, LANES), F32),
            vmem((STEPS, CHUNKS, DEVS + 2, 16, LANES), F32),
            vmem((1, STEPS, LANES), F32),
            vmem((DEVS, STEPS, LANES), F32),
            dma((9,)),
            dma((STEPS, CHUNKS)),
            dma((STEPS, CHUNKS, GROUPS)),
            dma((STEPS, CHUNKS, 2)),
            dma((STEPS, CHUNKS, 2)),
            dma,
            dma,
            pltpu.SemaphoreType.REGULAR,
        ],
        compiler_params=pltpu.CompilerParams(
            collective_id=0, has_side_effects=True, vmem_limit_bytes=40 << 20
        ),
        name="adjoint_steps",
    )(
        *[pltpu.with_memory_space_constraint(x, pltpu.HBM) for x in (psi.T, source.T, coupling.transpose(1, 2, 3, 0), diag_inv.transpose(1, 2, 0), neighbours.T,
        seam_perm, fringe_src, fringe_dst, fringe_weight)]
    )
    return results[0].T, results[1].T


def solution(mesh):
    rows = P(("body", "blk"))
    return jax.shard_map(
        shards,
        mesh=mesh,
        in_specs=(rows, rows, rows, rows, rows, P("body"), rows, rows, rows),
        out_specs=(rows, rows),
        check_vma=False,
    )
```

```python
import math

import jax
import jax.numpy as jnp
from jax import lax
from jax.experimental import pallas as pl
from jax.experimental.pallas import tpu as pltpu
from jax.sharding import PartitionSpec as P

CELLS = 64
VARS = 5
BW = 320
NB = 512
SLOTS = 6
RIM = 8
CAP = 8
GROUPS = 4
GROUP = 32
BODIES = 8
BLKS = 16
DEVS = 128
CHUNKS = 2
CC = CELLS // CHUNKS
CU = VARS * CC
ROWS = CU * CAP // 128
STEPS = 2
CFL = 0.5
LANES = 128
TILES = NB // LANES
TOTAL = DEVS * NB * BW
MESH = pl.DeviceIdType.MESH
F32 = jnp.float32
BF16 = jnp.bfloat16


def iota(shape, dim):
    return lax.broadcasted_iota(jnp.int32, shape, dim)


def split(x):
    hi = x.astype(BF16)
    return jnp.concatenate([hi, (x - hi.astype(F32)).astype(BF16)], axis=0)


def fold(y):
    return y[: y.shape[0] // 2] + y[y.shape[0] // 2 :]


def dot(a, b):
    return fold(jnp.dot(a, b, preferred_element_type=F32))


def dot_t(a, b):
    return fold(lax.dot_general(a, b, (((1,), (1,)), ((), ())), preferred_element_type=F32))


def device(o):
    return (lax.div(o, BLKS), lax.rem(o, BLKS))


def far_first(b, k):
    y, core, z, x = lax.div(b, 2), lax.rem(b, 2), lax.div(k, 4), lax.rem(k, 4)
    bodies = {(i, j): lax.rem(y + i, 4) * 2 + lax.rem(core + j, 2) for i in range(4) for j in range(2)}
    blks = {(i, j): lax.rem(z + i, 4) * 4 + lax.rem(x + j, 4) for i in range(4) for j in range(4)}
    steps = [(p, q) for p in bodies for q in blks if any(p + q)]
    hops = (0, 1, 2, 1)
    steps.sort(key=lambda s: -(hops[s[0][0]] + hops[s[1][0]] + hops[s[1][1]]))
    return [(bodies[p], blks[q]) for p, q in steps]


def kernel(
    psi_hbm, src_hbm, coup_hbm, dinv_hbm, nbr_hbm, perm_hbm, fsrc_hbm, fdst_hbm, fw_hbm,
    results,
    psi, src, coup, dinv, nbr, perm, fsrc, fdst, fw,
    sel, tab, near_hot, const, rim_hot,
    halves, halo, near, base, fringe, prec,
    out, inc, sums, total,
    lsem, ssem, rsem, rim_ssem, rim_rsem, sum_ssem, sum_rsem, row_sem,
):
    b, k = lax.axis_index("body"), lax.axis_index("blk")
    me = b * BLKS + k
    adj, res = results.at[0], results.at[1]
    group = lax.div(me, GROUP)
    nxt, prv = lax.rem(k + 1, BLKS), lax.rem(k + BLKS - 1, BLKS)

    loads = [
        pltpu.make_async_copy(s, d, lsem.at[i])
        for i, (s, d) in enumerate(
            [(psi_hbm, psi), (fsrc_hbm, fsrc), (nbr_hbm, nbr), (perm_hbm, perm), (fdst_hbm, fdst), (fw_hbm, fw),
             (src_hbm, src), (dinv_hbm, dinv), (coup_hbm, coup)]
        )
    ]
    for c in loads:
        c.start()

    bar = pltpu.get_barrier_semaphore()

    def greet_row(i, carry):
        pl.semaphore_signal(bar, inc=1, device_id=(b, lax.rem(k + i, BLKS)), device_id_type=MESH)
        return carry

    def tell_column(sem):
        def one(i, carry):
            pl.semaphore_signal(sem, inc=1, device_id=(lax.rem(b + i, BODIES), k), device_id_type=MESH)
            return carry

        lax.fori_loop(1, BODIES, one, 0)

    lax.fori_loop(1, BLKS, greet_row, 0)
    tell_column(bar)

    def slab(ref, s, c, first, count):
        return ref.at[s, c, pl.ds(first, count), pl.ds(0, ROWS)]

    def halve(c):
        for v in range(VARS):
            both = split(psi[v * CELLS + c * CC : v * CELLS + (c + 1) * CC, :])
            halves[c, v * CC : (v + 1) * CC, :] = both[:CC]
            halves[c, CU + v * CC : CU + (v + 1) * CC, :] = both[CC:]

    def pack(y):
        n = y.shape[1]
        main = y[:LANES].T.reshape(n // CAP, CAP, LANES)
        rem = y[LANES:]
        parts = [rem] + [pltpu.roll(rem, n - 2 * g, 1) for g in range(1, 4)]
        rest = jnp.concatenate(parts, axis=0).T.reshape(n // CAP, CAP, LANES)
        return main, rest

    def unpack(main, rest):
        n = main.shape[0] * CAP
        top = main.reshape(n, LANES).T
        x = rest.reshape(n, LANES).T
        group = lax.rem(iota((CC, n), 1), CAP) // 2
        low = x[:CC]
        for g in range(1, 4):
            low = jnp.where(group == g, pltpu.roll(x[g * CC : (g + 1) * CC], 2 * g, 1), low)
        return jnp.concatenate([top, low], axis=0)

    def rims(s, c):
        y = dot(halves[c], const[...])
        halo[c] = y[:, LANES:]
        main, rest = pack(y[:, :LANES])
        out[s, c, DEVS : DEVS + 2, 0:8] = main[:2]
        out[s, c, DEVS : DEVS + 2, 8:16] = rest[:2]

    def rim_copies(s, c):
        return [
            pltpu.make_async_remote_copy(
                slab(out, s, c, DEVS + i, 1), slab(inc, s, c, DEVS + i, 1),
                rim_ssem.at[s, c, i], rim_rsem.at[s, c, i],
                device_id=(b, to), device_id_type=MESH,
            )
            for i, to in enumerate((nxt, prv))
        ]

    def donors(s, c):
        def block(t, carry):
            cols = pl.ds(pl.multiple_of(t * 256, 256), 256)
            y = dot(halves[c], sel[:, cols])
            main, rest = pack(y)
            out[s, c, pl.ds(t * 32, 32), 0:8] = main
            out[s, c, pl.ds(t * 32, 32), 8:16] = rest
            return carry

        lax.fori_loop(0, 4, block, 0)
        inc[s, c, pl.ds(me, 1)] = out[s, c, pl.ds(me, 1)]

    def send_rims(s, c):
        for r in rim_copies(s, c):
            r.start()

    def send_to(s, c, i):
        o = me + i
        o = jnp.where(o >= DEVS, o - DEVS, o)
        pltpu.make_async_remote_copy(
            slab(out, s, c, o, 1), slab(inc, s, c, me, 1), ssem.at[s, c], rsem.at[s, c, group],
            device_id=o, device_id_type=pl.DeviceIdType.LOGICAL,
        ).start()

    def send(s, c):
        def one(i, carry):
            send_to(s, c, i)
            return carry

        lax.fori_loop(1, DEVS, one, 0)

    def wait_rims(s, c):
        for r in rim_copies(s, c):
            r.wait_recv()

    def wait_group(s, c, g, count):
        ref = slab(inc, s, c, 0, count)
        pltpu.make_async_copy(ref, ref, rsem.at[s, c, g]).wait()

    def wait_sends(s, c):
        ref = slab(out, s, c, 0, DEVS - 1)
        pltpu.make_async_copy(ref, ref, ssem.at[s, c]).wait()
        for r in rim_copies(s, c):
            r.wait_send()

    def couple(s, c, sends=None):
        wait_rims(s, c)
        zero = jnp.zeros((14, CAP, LANES), F32)
        main = jnp.concatenate([inc[s, c, DEVS : DEVS + 2, 0:8], zero], axis=0)
        rest = jnp.concatenate([inc[s, c, DEVS : DEVS + 2, 8:16], zero], axis=0)
        edge = halo[c] + dot(split(unpack(main, rest)), rim_hot[...])
        lane = iota((1, LANES), 1)
        turn_lo = (lane < RIM) & (k == 0)
        turn_hi = (lane >= 56) & (lane < 64) & (k == BLKS - 1)
        cosine = jnp.where(turn_lo | turn_hi, math.cos(2.0 * math.pi / 3.0), 1.0)
        sine = math.sin(2.0 * math.pi / 3.0)
        sine = jnp.where(turn_lo, sine, jnp.where(turn_hi, -sine, 0.0))
        e2, e3 = edge[2 * CC : 3 * CC], edge[3 * CC : 4 * CC]
        edge = jnp.concatenate(
            [edge[: 2 * CC], cosine * e2 - sine * e3, sine * e2 + cosine * e3, edge[4 * CC :]], axis=0
        )
        edge = split(edge)

        def tile(t, carry):
            cols = pl.ds(pl.multiple_of(t * LANES, LANES), LANES)
            near[...] = dot(jnp.concatenate([halves[c, :, cols], edge], axis=1), near_hot[t])
            if sends:
                send_to(*sends, t * GROUP + 1)
            acc = jnp.zeros((VARS, CC, LANES), F32)
            for v in range(VARS):
                rows = slice(v * CELLS + c * CC, v * CELLS + (c + 1) * CC)
                for m in range(SLOTS):
                    if sends:
                        send_to(*sends, t * GROUP + 2 + v * SLOTS + m)
                    x = near[v * CC : (v + 1) * CC, m * LANES : (m + 1) * LANES]
                    acc = acc + coup[m, :, rows, cols].astype(F32) * x[None]
            for v in range(VARS):
                rows = slice(v * CELLS + c * CC, v * CELLS + (c + 1) * CC)
                base[c, v * CC : (v + 1) * CC, cols] = src[rows, cols] - psi[rows, cols] + acc[v]
            if sends:

                @pl.when(t < TILES - 1)
                def _():
                    send_to(*sends, t * GROUP + GROUP)

            return carry

        lax.fori_loop(0, TILES, tile, 0)

    def gather_fringe(s, c):
        def block(g):
            cols = pl.ds(pl.multiple_of(g * 256, 256), 256)
            x = unpack(inc[s, c, pl.ds(g * GROUP, GROUP), 0:8], inc[s, c, pl.ds(g * GROUP, GROUP), 8:16])
            return dot_t(split(x * fw[:, cols]), tab[:, cols])

        def other(i, carry):
            g = lax.rem(group + GROUPS - i, GROUPS)
            wait_group(s, c, g, GROUP)
            fringe[...] += block(g)
            return carry

        before = lax.rem(group + GROUPS - 1, GROUPS)
        wait_group(s, c, before, GROUP)
        fringe[...] = block(before)
        lax.fori_loop(2, GROUPS, other, 0)
        wait_group(s, c, group, GROUP - 1)
        fringe[...] += block(group)

    def residual(s, c, square):
        def tile(t, square):
            cols = pl.ds(pl.multiple_of(t * LANES, LANES), LANES)
            acc = jnp.zeros((VARS, CC, LANES), F32)
            for v in range(VARS):
                rows = slice(v * CELLS + c * CC, v * CELLS + (c + 1) * CC)
                own = slice(v * CC, (v + 1) * CC)
                r = base[c, own, cols] + fringe[own, cols]
                square = square + jnp.sum((r * r).reshape(CC // 8, 8, LANES), axis=0)
                if s == STEPS - 1:
                    res[rows, cols] = r
                else:
                    acc = acc + dinv[:, rows, cols].astype(F32) * r[None]
            if s < STEPS - 1:
                for v in range(VARS):
                    rows = slice(v * CELLS + c * CC, v * CELLS + (c + 1) * CC)
                    psi[rows, cols] = psi[rows, cols] + CFL * acc[v]
            return square

        return lax.fori_loop(0, TILES, tile, square)

    loads[0].wait()
    loads[1].wait()
    halve(0)
    tgt = iota((1, 2 * LANES), 1)
    h = tgt - LANES
    t, e = h // 16, lax.rem(h, 16)
    own = jnp.where(e < RIM, LANES * t - RIM + e, LANES * (t + 1) + e - RIM)
    own = jnp.where(h < 64, own, -1)
    rim = jnp.where(tgt < RIM, NB - RIM + tgt, jnp.where(tgt < 2 * RIM, tgt - RIM, -1))
    tgt = jnp.where(tgt < LANES, rim, own)

    def build(i, carry):
        at = pl.multiple_of(i * 64, 64)
        row = iota((64, DEVS * CAP), 0) + at
        sel[pl.ds(at, 64)] = jnp.where(row == fsrc[...], 1.0, 0.0).astype(BF16)
        const[pl.ds(at, 64)] = jnp.where(row[:, : 2 * LANES] == tgt, 1.0, 0.0).astype(BF16)
        return carry

    lax.fori_loop(0, NB // 64, build, 0)
    pl.semaphore_wait(bar, BLKS - 1 + BODIES - 1)
    tell_column(row_sem)
    rims(0, 0)
    donors(0, 0)
    pl.semaphore_wait(row_sem, BODIES - 1)
    send_rims(0, 0)
    send(0, 0)
    halve(1)
    rims(0, 1)
    send_rims(0, 1)
    donors(0, 1)

    for c in loads[2:6]:
        c.wait()

    def build_in(i, carry):
        at = pl.multiple_of(i * 64, 64)
        row = iota((64, DEVS * CAP), 0) + at
        tab[pl.ds(at, 64)] = jnp.where(row == fdst[...], 1.0, 0.0).astype(BF16)
        return carry

    lax.fori_loop(0, NB // 64, build_in, 0)
    row = iota((2 * LANES, LANES), 0)
    for t in range(TILES):
        for m in range(SLOTS):
            d = nbr[m : m + 1, t * LANES : (t + 1) * LANES] - (RIM + t * LANES)
            d = jnp.where(d < 0, d + (LANES + 16 * t + RIM), jnp.where(d >= LANES, d + (16 * t + RIM), d))
            near_hot[t, :, m * LANES : (m + 1) * LANES] = jnp.where(row == d, 1.0, 0.0).astype(BF16)
    row, col = iota((LANES, LANES), 0), iota((LANES, LANES), 1)
    hot = jnp.zeros((LANES, LANES), F32)
    for j in range(RIM):
        p = perm[0, j]
        low = jnp.where(k == 0, p, j)
        high = jnp.where(k == BLKS - 1, p, j) + 56
        hot = jnp.where((row == low) & (col == j), 1.0, hot)
        hot = jnp.where((row == RIM + j) & (col == high), 1.0, hot)
    rim_hot[...] = hot.astype(BF16)
    for c in loads[6:]:
        c.wait()

    square = [jnp.zeros((8, LANES), F32) for _ in range(STEPS)]
    order = [(s, c) for s in range(STEPS) for c in range(CHUNKS)]
    pending = (0, 1)
    for s, c in order:
        couple(s, c, pending)
        pending = None
        gather_fringe(s, c)
        square[s] = residual(s, c, square[s])
        if s < STEPS - 1:
            halve(c)
            rims(s + 1, c)
            send_rims(s + 1, c)
            donors(s + 1, c)
            pending = (s + 1, c)

    sums[...] = jnp.concatenate([jnp.sum(x, axis=0, keepdims=True) for x in square], axis=0)[None]
    total[pl.ds(me, 1)] = sums[...]

    for to in far_first(b, k):
        pltpu.make_async_remote_copy(
            sums.at[0], total.at[me], sum_ssem, sum_rsem, device_id=to, device_id_type=MESH
        ).start()

    def precondition(i, carry):
        c, t = lax.div(i, TILES), lax.rem(i, TILES)
        cols = pl.ds(pl.multiple_of(t * LANES, LANES), LANES)
        acc = jnp.zeros((VARS, CC, LANES), F32)
        for v in range(VARS):
            rows = pl.ds(pl.multiple_of(v * CELLS + c * CC, CC), CC)
            acc = acc + dinv[:, rows, cols].astype(F32) * res[rows, cols][None]
        for v in range(VARS):
            prec[pl.ds(pl.multiple_of(v * CELLS + c * CC, CC), CC), cols] = acc[v]
        return carry

    lax.fori_loop(0, CHUNKS * TILES, precondition, 0)
    ref = total.at[pl.ds(0, DEVS - 1)]
    pltpu.make_async_copy(ref, ref, sum_rsem).wait()
    q = jnp.sum(jnp.sum(total[...], axis=0), axis=1, keepdims=True) * (1.0 / TOTAL) + 1e-06
    cfl = CFL * jnp.sqrt(q[0:1] / q[1:2])

    def last(i, carry):
        rows = pl.ds(pl.multiple_of(i * 32, 32), 32)
        adj[rows] = psi[rows] + cfl * prec[rows]
        return carry

    lax.fori_loop(0, BW // 32, last, 0)
    pltpu.make_async_copy(ref, ref, sum_ssem).wait()
    for s in range(STEPS):
        for c in range(CHUNKS):
            wait_sends(s, c)


def shards(psi, source, coupling, diag_inv, neighbours, seam_perm, fringe_src, fringe_dst, fringe_weight):
    any_space = pl.BlockSpec(memory_space=pl.ANY)
    vmem = pltpu.VMEM
    dma = pltpu.SemaphoreType.DMA
    slots = DEVS * CAP
    results = pl.pallas_call(
        kernel,
        out_shape=jax.ShapeDtypeStruct((2, BW, NB), F32),
        in_specs=[any_space] * 9,
        out_specs=pl.BlockSpec(memory_space=vmem),
        scratch_shapes=[
            vmem((BW, NB), F32),
            vmem((BW, NB), F32),
            vmem((SLOTS, VARS, BW, NB), BF16),
            vmem((VARS, BW, NB), BF16),
            vmem((SLOTS, NB), jnp.int32),
            pltpu.SMEM((1, RIM), jnp.int32),
            vmem((1, slots), jnp.int32),
            vmem((1, slots), jnp.int32),
            vmem((1, slots), F32),
            vmem((NB, slots), BF16),
            vmem((NB, slots), BF16),
            vmem((TILES, 2 * LANES, SLOTS * LANES), BF16),
            vmem((NB, 2 * LANES), BF16),
            vmem((LANES, LANES), BF16),
            vmem((CHUNKS, 2 * CU, NB), BF16),
            vmem((CHUNKS, CU, LANES), F32),
            vmem((CU, SLOTS * LANES), F32),
            vmem((CHUNKS, CU, NB), F32),
            vmem((CU, NB), F32),
            vmem((BW, NB), F32),
            vmem((STEPS, CHUNKS, DEVS + 2, 16, LANES), F32),
            vmem((STEPS, CHUNKS, DEVS + 2, 16, LANES), F32),
            vmem((1, STEPS, LANES), F32),
            vmem((DEVS, STEPS, LANES), F32),
            dma((9,)),
            dma((STEPS, CHUNKS)),
            dma((STEPS, CHUNKS, GROUPS)),
            dma((STEPS, CHUNKS, 2)),
            dma((STEPS, CHUNKS, 2)),
            dma,
            dma,
            pltpu.SemaphoreType.REGULAR,
        ],
        compiler_params=pltpu.CompilerParams(
            collective_id=0, has_side_effects=True, vmem_limit_bytes=40 << 20
        ),
        name="adjoint_steps",
    )(
        *[pltpu.with_memory_space_constraint(x, pltpu.HBM) for x in (psi.T, source.T, coupling.transpose(1, 2, 3, 0), diag_inv.transpose(1, 2, 0), neighbours.T,
        seam_perm, fringe_src, fringe_dst, fringe_weight)]
    )
    return results[0].T, results[1].T


def solution(mesh):
    rows = P(("body", "blk"))
    return jax.shard_map(
        shards,
        mesh=mesh,
        in_specs=(rows, rows, rows, rows, rows, P("body"), rows, rows, rows),
        out_specs=(rows, rows),
        check_vma=False,
    )
```
